1024 devices in a mesh: ctx: 64 (over z, x_hi, core), head: 16 (over x_lo, y).
Axes of the slice: x: 4 (x_hi: 2, x_lo: 2; x = x_hi * 2 + x_lo), y: 8, z: 16, core: 2. Of those that a mesh axis runs over, the one named last changes fastest.
Arguments:
- tokens: bfloat16 [16384, 2048], P('ctx'), may hold values from -15 to 15
- w_qkv: bfloat16 [3, 2048, 2048], P(None, None, 'head'), may hold values from -0.9943689 to 0.9943689
- w_out: bfloat16 [2048, 2048], P('head'), may hold values from -0.125 to 0.125
- w_dec: bfloat16 [2048, 12, 256], P(None, None, 'head'), may hold values from -0.125 to 0.125
Outputs:
- field: float32 [16384, 8, 256], P('ctx', None, 'head')
The draws below stay inside these ranges and needn't reach their ends.
All inputs are finite; a program needn't handle non-finite values.
Results may differ from the reference program's by a relative error of at most 0.011.
Values may be sent and summed in bfloat16 or wider, within the bound.
A program may use at most 32 MiB of HBM per device.

```python
import math
import jax
import jax.numpy as jnp
from jax import lax

D = 2048
HEADS = 32
HD = 64
PATCH = 8
OV = 2
TOK_DEV = 256
TOKENS = 16384
XE = 12
CELLS = 256


def draw_tokens(key, part):
    first = jax.random.fold_in(key, 11)
    second = jax.random.fold_in(key, 12)
    columns = jnp.exp(jax.random.uniform(second, (D,), jnp.float32) * math.log(10.0)) / 4.0
    values = jnp.clip(jax.random.normal(first, (TOKENS, D), jnp.float32), -6.0, 6.0) * columns[None, :]
    return values.astype(jnp.bfloat16)


def draw_w_qkv(key, part):
    first = jax.random.fold_in(key, 21)
    width = HEADS * HD
    base = jnp.clip(jax.random.normal(first, (3, D, width), jnp.float32), -6.0, 6.0) * D ** (-0.5)
    stacked = base * jnp.array([3.0, 1.0, 1.0], jnp.float32).reshape(3, 1, 1)
    return stacked.astype(jnp.bfloat16)


def shard_levels(stream_key, extent, shards, least, high):
    factor_of = 1.0
    for dim, parts in shards:
        draws = jax.random.uniform(jax.random.fold_in(jax.random.fold_in(stream_key, 6), dim), (parts,), jnp.float32, least / len(shards), high / len(shards))
        factor_of = factor_of * jnp.repeat(jnp.exp(draws), extent[dim] // parts).reshape((-1,) + (1,) * (len(extent) - 1 - dim))
    return factor_of


def gaussian(key, shape, scale, bound, shards=(), held_as=jnp.bfloat16):
    entries = jax.random.normal(key, shape, jnp.float32) * scale
    if len(shards) > 0:
        entries = shard_levels(key, shape, shards, -0.22, 0.18) * entries
    return jnp.clip(entries, min=-bound, max=bound).astype(held_as)


def setup_inputs(seed: int = 0) -> dict:
    seeds = jax.random.split(jax.random.key(seed), 5)
    return {
        "tokens": draw_tokens(jax.random.fold_in(seeds[4], 71), 0),
        "w_qkv": draw_w_qkv(jax.random.fold_in(seeds[4], 71), 0),
        "w_out": gaussian(seeds[2], (HEADS * HD, D), (HEADS * HD) ** -0.5, 0.125, ((0, 16),)),
        "w_dec": gaussian(seeds[3], (D, XE, CELLS), D ** -0.5, 0.125, ((2, 16),)),
    }


def rms_scale(values):
    return values * lax.rsqrt(lax.optimization_barrier(jnp.mean(values * values, axis=-1, keepdims=True)) + 1e-05)

def reference(tokens, w_qkv, w_out, w_dec):
    xf = tokens.astype(jnp.float32)
    normed = rms_scale(xf).astype(jnp.bfloat16)
    projected = jnp.einsum('td,kdc->ktc', normed.astype(jnp.float32), w_qkv.astype(jnp.float32)).astype(jnp.bfloat16)
    queries = projected[0].reshape(TOKENS, HEADS, HD).transpose(1, 0, 2)
    keys = projected[1].reshape(TOKENS, HEADS, HD).transpose(1, 0, 2)
    values = projected[2].reshape(TOKENS, HEADS, HD).transpose(1, 0, 2)
    span = math.gcd(TOKENS, 1024)
    scale = HD ** (-0.5)

    def one_head(items):
        head_q, head_k, head_v = items

        def one_block(block_q):
            scores = jnp.dot(block_q, head_k.T, preferred_element_type=jnp.float32) * scale
            top = lax.optimization_barrier(jnp.max(scores, axis=-1, keepdims=True))
            weights = jnp.exp(scores - top)
            total = lax.optimization_barrier(jnp.sum(weights, axis=-1, keepdims=True))
            summed = jnp.dot(weights.astype(jnp.bfloat16), head_v, preferred_element_type=jnp.float32)
            return summed / total
        return lax.map(one_block, head_q.reshape(TOKENS // span, span, HD)).reshape(TOKENS, HD)
    attended = lax.map(one_head, (queries, keys, values))
    attended = attended.transpose(1, 0, 2).reshape(TOKENS, HEADS * HD).astype(jnp.bfloat16)
    mixed = jnp.dot(attended, w_out, preferred_element_type=jnp.float32)
    hidden = rms_scale(xf + mixed).astype(jnp.bfloat16)
    extended = jnp.dot(hidden, w_dec.reshape(D, XE * CELLS), preferred_element_type=jnp.float32).reshape(TOKENS, XE, CELLS)
    before = jnp.roll(extended, TOK_DEV, axis=0)
    after = jnp.roll(extended, -TOK_DEV, axis=0)
    field = jnp.concatenate([extended[:, OV:2 * OV] + before[:, PATCH + OV:], extended[:, 2 * OV:PATCH], extended[:, PATCH:PATCH + OV] + after[:, :OV]], axis=1)
    return field
```

```python
import functools

import jax
import jax.numpy as jnp
from jax import lax
from jax.experimental import pallas as pl
from jax.experimental.pallas import tpu as pltpu
from jax.sharding import PartitionSpec as P

HD = 64
PATCH = 8
OV = 2
EPS = 1e-05
LOG2E = 1.4426950408889634
F32 = jnp.float32
BF16 = jnp.bfloat16


def nt(a, b):
    return lax.dot_general(a, b, (((1,), (1,)), ((), ())), preferred_element_type=F32)


def nn(a, b):
    return jnp.dot(a, b, preferred_element_type=F32)


def kernel(
    n_ctx,
    n_head,
    tok_hbm,
    wqkv_hbm,
    wout_hbm,
    wdec_hbm,
    out_ref,
    tok,
    wqkv,
    wout,
    wdec,
    wout_t,
    wcol_t,
    q_raw,
    q_pad,
    kbuf,
    vbuf,
    m_ref,
    l_ref,
    acc,
    part_send,
    stat_send,
    part_recv,
    stat_recv,
    att,
    hid,
    halo_send,
    halo_recv,
    load_sem,
    own_send,
    k_send,
    v_send,
    k_recv,
    v_recv,
    q_send,
    q_recv,
    w_send,
    w_recv,
    c_send,
    c_recv,
    st_send,
    st_recv,
    g_recv,
    g_pos,
    g_neg,
    g_pair,
    halo_ssem,
    halo_rsem,
):
    rows, width = tok.shape
    nz, ny = n_ctx // 4, n_head // 2
    last = nz - 1
    cols = 2 * HD
    cells = PATCH * 16

    ctx = lax.axis_index("ctx")
    head = lax.axis_index("head")
    core = ctx % 2
    xh = (ctx // 2) % 2
    z = ctx // 4
    xl = head // ny
    y = head % ny
    mine = xh * 2 + core
    up = (z + 1) % nz
    down = (z + nz - 1) % nz
    dev_up = (up * 4 + xh * 2, head)
    dev_down = (down * 4 + xh * 2 + 1, head)

    def remote(src, dst, ssem, rsem, device):
        return pltpu.make_async_remote_copy(
            src_ref=src,
            dst_ref=dst,
            send_sem=ssem,
            recv_sem=rsem,
            device_id=device,
            device_id_type=pl.DeviceIdType.MESH,
        )

    loads = [
        pltpu.make_async_copy(a, b, load_sem.at[i])
        for i, (a, b) in enumerate(
            ((tok_hbm, tok), (wqkv_hbm, wqkv), (wout_hbm, wout), (wdec_hbm, wdec))
        )
    ]
    for load in loads:
        load.start()

    barrier = pltpu.get_barrier_semaphore()

    def greet(device):
        pl.semaphore_signal(
            barrier, inc=1, device_id=device, device_id_type=pl.DeviceIdType.MESH
        )

    source_z = (z + nz - 1 + 2 * core) % nz
    greet((source_z * 4 + xh * 2, head))
    greet((source_z * 4 + xh * 2 + 1, head))
    for step in range(1, 4):
        other = (mine + step) % 4
        greet((z * 4 + other, head))

    @pl.loop(1, n_head)
    def _(step):
        greet((ctx, (head + step) % n_head))

    greet(((ctx + 1) % n_ctx, head))
    greet(((ctx + n_ctx - 1) % n_ctx, head))

    loads[0].wait()
    x = tok[...]
    xf = x.astype(F32)
    r = lax.rsqrt(jnp.mean(xf * xf, axis=-1, keepdims=True) + EPS)
    loads[1].wait()
    kbuf[0] = (nn(x, wqkv[1]) * r).astype(BF16)
    vbuf[0] = (nn(x, wqkv[2]) * r).T.astype(BF16)
    pl.semaphore_wait(barrier, n_head + 6)

    first = []
    for t, device in enumerate((dev_up, dev_down)):
        first.append(
            remote(kbuf.at[0], kbuf.at[1 + core], own_send.at[2 * t], k_recv.at[1 + core], device)
        )
        first.append(
            remote(
                vbuf.at[0], vbuf.at[1 + core], own_send.at[2 * t + 1], v_recv.at[1 + core], device
            )
        )
    for copy in first:
        copy.start()

    q_raw[mine] = (nn(x, wqkv[0]) * (r * (HD**-0.5 * LOG2E))).astype(BF16)
    q_copies = []
    for step in (2, 1, 3):
        other = (mine + step) % 4
        q_copies.append(
            remote(
                q_raw.at[mine], q_raw.at[mine], q_send.at[step], q_recv.at[mine], (z * 4 + other, head)
            )
        )
    for copy in q_copies:
        copy.start()

    def forward(j, buf, ssem, rsem):
        target = jnp.minimum(j + 2, last)
        return remote(
            buf.at[j],
            buf.at[target],
            ssem.at[j],
            rsem.at[target],
            ((z + 1 + core * (nz - 2)) % nz * 4 + xh * 2 + core, head),
        )

    def passes_on(j):
        return jnp.logical_or(j <= last - 3, j == last - 2 + core)

    def arrive(j):
        for buf, ssem, rsem in ((kbuf, k_send, k_recv), (vbuf, v_send, v_recv)):
            remote(buf.at[j], buf.at[j], ssem.at[j], rsem.at[j], dev_up).wait_recv()

            @pl.when(passes_on(j))
            def _():
                forward(j, buf, ssem, rsem).start()

    loads[2].wait()
    wout_t[...] = wout[...].astype(F32).T.astype(BF16)
    wcol_t[head] = wout_t[pl.ds(pl.multiple_of(head * cols, cols), cols), :]

    def w_copy(step):
        other = (head + step) % n_head
        return remote(
            wout_t.at[pl.ds(pl.multiple_of(other * cols, cols), cols), :],
            wcol_t.at[head],
            w_send.at[step],
            w_recv.at[head],
            (ctx, other),
        )

    @pl.loop(1, n_head)
    def _(step):
        w_copy(step).start()

    arrive(1)

    m_ref[...] = jnp.full_like(m_ref, -1e30)
    l_ref[...] = jnp.zeros_like(l_ref)
    acc[...] = jnp.zeros_like(acc)
    for step in range(1, 4):
        other = (mine + step) % 4
        remote(
            q_raw.at[other], q_raw.at[other], q_send.at[step], q_recv.at[other], dev_up
        ).wait_recv()
    low = lax.broadcasted_iota(jnp.int32, (rows, cols), 1) < HD
    for b in range(4):
        q = q_raw[b]
        zero = jnp.zeros_like(q)
        q_pad[0, b * rows : (b + 1) * rows, :] = jnp.where(low, q, zero)
        q_pad[1, b * rows : (b + 1) * rows, :] = jnp.where(low, zero, q)

    def attend(j):
        keys = kbuf[j]
        values = vbuf[j]
        for h in range(2):
            for part in range(2):
                span = slice(part * 2 * rows, (part + 1) * 2 * rows)
                scores = nt(keys, q_pad[h, span, :])
                old = m_ref[h : h + 1, span]
                new = jnp.maximum(old, jnp.max(scores, axis=0, keepdims=True))
                weights = jnp.exp2(scores - new)
                shrink = jnp.exp2(old - new)
                m_ref[h : h + 1, span] = new
                l_ref[h : h + 1, span] = l_ref[h : h + 1, span] * shrink + jnp.sum(
                    weights, axis=0, keepdims=True
                )
                acc[h, :, span] = acc[h, :, span] * shrink + nn(
                    values[h * HD : (h + 1) * HD, :], weights.astype(BF16)
                )

    @pl.loop(1, nz + 1)
    def _(j):
        @pl.when(jnp.logical_and(j >= 2, j <= last))
        def _():
            arrive(j)

        attend(j - 1)

    c_copies = []
    for step in (2, 1, 3):
        other = (mine + step) % 4
        span = pl.ds(pl.multiple_of(other * rows, rows), rows)
        for h in range(2):
            part_send[other, h * HD : (h + 1) * HD, :] = acc[h, :, span].astype(BF16)
            stat_send[other, h : h + 1, :] = m_ref[h : h + 1, span]
            stat_send[other, 2 + h : 3 + h, :] = l_ref[h : h + 1, span]
        device = (z * 4 + other, head)
        c_copies.append(
            remote(part_send.at[other], part_recv.at[mine], c_send.at[step], c_recv.at[mine], device)
        )
        c_copies.append(
            remote(
                stat_send.at[other], stat_recv.at[mine], st_send.at[step], st_recv.at[mine], device
            )
        )
        c_copies[-2].start()
        c_copies[-1].start()

    @pl.loop(1, last)
    def _(j):
        @pl.when(passes_on(j))
        def _():
            forward(j, kbuf, k_send, k_recv).wait_send()
            forward(j, vbuf, v_send, v_recv).wait_send()

    for copy in first + q_copies:
        copy.wait_send()

    for step in range(1, 4):
        other = (mine + step) % 4
        remote(
            part_recv.at[other], part_recv.at[other], c_send.at[step], c_recv.at[other], dev_up
        ).wait_recv()
        remote(
            stat_recv.at[other], stat_recv.at[other], st_send.at[step], st_recv.at[other], dev_up
        ).wait_recv()
    span = pl.ds(pl.multiple_of(mine * rows, rows), rows)
    for h in range(2):
        tops = [m_ref[h : h + 1, span]]
        sums = [l_ref[h : h + 1, span]]
        parts = [acc[h, :, span]]
        for step in range(1, 4):
            other = (mine + step) % 4
            tops.append(stat_recv[other, h : h + 1, :])
            sums.append(stat_recv[other, 2 + h : 3 + h, :])
            parts.append(part_recv[other, h * HD : (h + 1) * HD, :].astype(F32))
        top = functools.reduce(jnp.maximum, tops)
        scales = [jnp.exp2(t - top) for t in tops]
        total = functools.reduce(jnp.add, [a * b for a, b in zip(scales, sums)])
        inverse = 1.0 / total
        mixed = functools.reduce(jnp.add, [(a * inverse) * b for a, b in zip(scales, parts)])
        att[head, h * HD : (h + 1) * HD, :] = mixed.astype(BF16)

    sign = 1 - 2 * core
    pair = (ctx, (1 - xl) * ny + y)
    pos = (ctx, xl * ny + (y + sign + ny) % ny)
    neg = (ctx, xl * ny + (y - sign + ny) % ny)

    def gather(which, buf, use):
        started = []

        def send(src, sems, device):
            copy = remote(
                buf.at[src], buf.at[src], sems.at[which, src], g_recv.at[which, src], device
            )
            copy.start()
            started.append(copy)

        def wait(src):
            remote(
                buf.at[src], buf.at[src], g_pos.at[which, src], g_recv.at[which, src], pos
            ).wait_recv()

        send(head, g_pair, pair)
        send(head, g_pos, pos)
        send(head, g_neg, neg)
        use(head)
        src = (1 - xl) * ny + y
        wait(src)
        send(src, g_pos, pos)
        use(src)
        half = ny // 2
        for d in range(1, half + 1):
            behind = (y - sign * d + ny) % ny
            ahead = (y + sign * d + ny) % ny
            if d < half:
                src = xl * ny + behind
                wait(src)
                if d < half - 1:
                    send(src, g_pos, pos)
            ahead_src = xl * ny + ahead
            wait(ahead_src)
            send(ahead_src, g_pair, pair)
            if d < half:
                send(ahead_src, g_neg, neg)
                use(src)
                far = (1 - xl) * ny + behind
                wait(far)
                if d < half - 1:
                    send(far, g_pos, pos)
                use(far)
            use(ahead_src)
            far = (1 - xl) * ny + ahead
            wait(far)
            use(far)
        return started

    residual = tok[:, pl.ds(pl.multiple_of(head * cols, cols), cols)].astype(F32).T

    @pl.loop(1, n_head)
    def _(step):
        other = (head + step) % n_head
        remote(
            wcol_t.at[other], wcol_t.at[other], w_send.at[step], w_recv.at[other], pos
        ).wait_recv()

    total = [residual]

    def project(src):
        total[0] = total[0] + nn(wcol_t[src], att[src])

    started = gather(0, att, project)
    hid[head] = total[0].astype(BF16)

    ext = [jnp.zeros((wdec.shape[0], rows), F32)]
    squares = [jnp.zeros((cols, rows), F32)]

    def decode(src):
        block = hid[src]
        wide = block.astype(F32)
        squares[0] = squares[0] + wide * wide
        ext[0] = ext[0] + nn(wdec[:, pl.ds(pl.multiple_of(src * cols, cols), cols)], block)

    loads[3].wait()
    started += gather(1, hid, decode)
    mean = jnp.sum(squares[0], axis=0, keepdims=True) * (1.0 / width)
    field = ext[0] * lax.rsqrt(mean + EPS)

    edge = OV * 16
    halo_send[0] = field[cells + edge :, :].astype(BF16)
    halo_send[1] = field[:edge, :].astype(BF16)
    halos = []
    for i, device in enumerate((((ctx + 1) % n_ctx, head), ((ctx + n_ctx - 1) % n_ctx, head))):
        halos.append(
            remote(halo_send.at[i], halo_recv.at[i], halo_ssem.at[i], halo_rsem.at[i], device)
        )
    for copy in halos:
        copy.start()
    out_ref[edge : cells - edge, :] = field[2 * edge : cells, :]
    for copy in started + c_copies:
        copy.wait_send()

    @pl.loop(1, n_head)
    def _(step):
        w_copy(step).wait_send()

    halos[0].wait()
    out_ref[:edge, :] = field[edge : 2 * edge, :] + halo_recv[0].astype(F32)
    halos[1].wait()
    out_ref[cells - edge :, :] = field[cells : cells + edge, :] + halo_recv[1].astype(F32)


def body(n_ctx, n_head, tokens, w_qkv, w_out, w_dec):
    rows, width = tokens.shape
    cols = w_qkv.shape[2]
    nz = n_ctx // 4
    wdec_t = jnp.transpose(w_dec, (1, 2, 0)).reshape(-1, width)
    cells = PATCH * w_dec.shape[2]
    dma = pltpu.SemaphoreType.DMA
    anywhere = pl.BlockSpec(memory_space=pl.ANY)
    flops = 2 * rows * width * (3 * cols + cols + wdec_t.shape[0])
    flops += 4 * (4 * rows) * (rows * nz) * cols
    out = pl.pallas_call(
        functools.partial(kernel, n_ctx, n_head),
        out_shape=jax.ShapeDtypeStruct((cells, rows), F32),
        in_specs=[anywhere] * 4,
        out_specs=pl.BlockSpec(memory_space=pltpu.VMEM),
        scratch_shapes=[
            pltpu.VMEM((rows, width), BF16),
            pltpu.VMEM(w_qkv.shape, BF16),
            pltpu.VMEM(w_out.shape, BF16),
            pltpu.VMEM(wdec_t.shape, BF16),
            pltpu.VMEM((width, cols), BF16),
            pltpu.VMEM((n_head, cols, cols), BF16),
            pltpu.VMEM((4, rows, cols), BF16),
            pltpu.VMEM((2, 4 * rows, cols), BF16),
            pltpu.VMEM((nz, rows, cols), BF16),
            pltpu.VMEM((nz, cols, rows), BF16),
            pltpu.VMEM((2, 4 * rows), F32),
            pltpu.VMEM((2, 4 * rows), F32),
            pltpu.VMEM((2, HD, 4 * rows), F32),
            pltpu.VMEM((4, cols, rows), BF16),
            pltpu.VMEM((4, 8, rows), F32),
            pltpu.VMEM((4, cols, rows), BF16),
            pltpu.VMEM((4, 8, rows), F32),
            pltpu.VMEM((n_head, cols, rows), BF16),
            pltpu.VMEM((n_head, cols, rows), BF16),
            pltpu.VMEM((2, 2 * OV * 8, rows), BF16),
            pltpu.VMEM((2, 2 * OV * 8, rows), BF16),
            dma((4,)),
            dma((4,)),
            dma((nz,)),
            dma((nz,)),
            dma((nz,)),
            dma((nz,)),
            dma((4,)),
            dma((4,)),
            dma((n_head,)),
            dma((n_head,)),
            dma((4,)),
            dma((4,)),
            dma((4,)),
            dma((4,)),
            dma((2, n_head)),
            dma((2, n_head)),
            dma((2, n_head)),
            dma((2, n_head)),
            dma((2,)),
            dma((2,)),
        ],
        compiler_params=pltpu.CompilerParams(
            collective_id=0, has_side_effects=True, vmem_limit_bytes=48 * 1024 * 1024
        ),
        cost_estimate=pl.CostEstimate(flops=flops, bytes_accessed=1 << 22, transcendentals=1 << 23),
        name="layer",
    )(tokens, w_qkv, w_out, wdec_t)
    return jnp.transpose(out.reshape(PATCH, w_dec.shape[2], rows), (2, 0, 1))


def solution(mesh):
    return jax.shard_map(
        functools.partial(body, mesh.shape["ctx"], mesh.shape["head"]),
        mesh=mesh,
        in_specs=(P("ctx", None), P(None, None, "head"), P("head", None), P(None, None, "head")),
        out_specs=P("ctx", None, "head"),
        check_vma=False,
    )
```

```python
import functools

import jax
import jax.numpy as jnp
from jax import lax
from jax.experimental import pallas as pl
from jax.experimental.pallas import tpu as pltpu
from jax.sharding import PartitionSpec as P

HD = 64
PATCH = 8
OV = 2
EPS = 1e-05
LOG2E = 1.4426950408889634
F32 = jnp.float32
BF16 = jnp.bfloat16


def nt(a, b):
    return lax.dot_general(a, b, (((1,), (1,)), ((), ())), preferred_element_type=F32)


def nn(a, b):
    return jnp.dot(a, b, preferred_element_type=F32)


def kernel(
    n_ctx,
    n_head,
    tok_hbm,
    wqkv_hbm,
    wout_hbm,
    wdec_hbm,
    out_ref,
    tok,
    wqkv,
    wout,
    wdec,
    wout_t,
    wcol_t,
    q_raw,
    q_pad,
    kbuf,
    vbuf,
    m_ref,
    l_ref,
    acc,
    part_send,
    stat_send,
    part_recv,
    stat_recv,
    att,
    hid,
    halo_send,
    halo_recv,
    load_sem,
    own_send,
    k_send,
    v_send,
    k_recv,
    v_recv,
    q_send,
    q_recv,
    w_send,
    w_recv,
    c_send,
    c_recv,
    st_send,
    st_recv,
    g_recv,
    g_pos,
    g_neg,
    g_pos2,
    g_neg2,
    g_pair,
    halo_ssem,
    halo_rsem,
):
    rows, width = tok.shape
    nz, ny = n_ctx // 4, n_head // 2
    last = nz - 1
    cols = 2 * HD
    cells = PATCH * 16

    ctx = lax.axis_index("ctx")
    head = lax.axis_index("head")
    core = ctx % 2
    xh = (ctx // 2) % 2
    z = ctx // 4
    xl = head // ny
    y = head % ny
    mine = xh * 2 + core
    up = (z + 1) % nz
    down = (z + nz - 1) % nz
    dev_up = (up * 4 + xh * 2, head)
    dev_down = (down * 4 + xh * 2 + 1, head)

    def remote(src, dst, ssem, rsem, device):
        return pltpu.make_async_remote_copy(
            src_ref=src,
            dst_ref=dst,
            send_sem=ssem,
            recv_sem=rsem,
            device_id=device,
            device_id_type=pl.DeviceIdType.MESH,
        )

    loads = [
        pltpu.make_async_copy(a, b, load_sem.at[i])
        for i, (a, b) in enumerate(
            ((tok_hbm, tok), (wqkv_hbm, wqkv), (wout_hbm, wout), (wdec_hbm, wdec))
        )
    ]
    for load in loads:
        load.start()

    barrier = pltpu.get_barrier_semaphore()

    def greet(device):
        pl.semaphore_signal(
            barrier, inc=1, device_id=device, device_id_type=pl.DeviceIdType.MESH
        )

    source_z = (z + nz - 1 + 2 * core) % nz
    greet((source_z * 4 + xh * 2, head))
    greet((source_z * 4 + xh * 2 + 1, head))
    for step in range(1, 4):
        other = (mine + step) % 4
        greet((z * 4 + other, head))

    @pl.loop(1, n_head)
    def _(step):
        greet((ctx, (head + step) % n_head))

    greet(((ctx + 1) % n_ctx, head))
    greet(((ctx + n_ctx - 1) % n_ctx, head))

    loads[0].wait()
    loads[1].wait()
    x = tok[...]
    xf = x.astype(F32)
    r = lax.rsqrt(jnp.mean(xf * xf, axis=-1, keepdims=True) + EPS)
    keyvals = nn(x, jnp.concatenate([wqkv[1], wqkv[2]], axis=1)) * r
    kbuf[0] = keyvals[:, :cols].astype(BF16)
    vbuf[0] = keyvals[:, cols:].T.astype(BF16)
    pl.semaphore_wait(barrier, n_head + 6)

    first = []
    for t, device in enumerate((dev_up, dev_down)):
        first.append(
            remote(kbuf.at[0], kbuf.at[1 + core], own_send.at[2 * t], k_recv.at[1 + core], device)
        )
        first.append(
            remote(
                vbuf.at[0], vbuf.at[1 + core], own_send.at[2 * t + 1], v_recv.at[1 + core], device
            )
        )
    for copy in first:
        copy.start()

    q_raw[mine] = (nn(x, wqkv[0]) * (r * (HD**-0.5 * LOG2E))).astype(BF16)
    q_copies = []
    for step in (2, 1, 3):
        other = (mine + step) % 4
        q_copies.append(
            remote(
                q_raw.at[mine], q_raw.at[mine], q_send.at[step], q_recv.at[mine], (z * 4 + other, head)
            )
        )
    for copy in q_copies:
        copy.start()

    def forward(j, buf, ssem, rsem):
        target = jnp.minimum(j + 2, last)
        return remote(
            buf.at[j],
            buf.at[target],
            ssem.at[j],
            rsem.at[target],
            ((z + 1 + core * (nz - 2)) % nz * 4 + xh * 2 + core, head),
        )

    def passes_on(j):
        return jnp.logical_or(j <= last - 3, j == last - 2 + core)

    def arrive(j, buf, ssem, rsem):
        remote(buf.at[j], buf.at[j], ssem.at[j], rsem.at[j], dev_up).wait_recv()

        @pl.when(passes_on(j))
        def _():
            forward(j, buf, ssem, rsem).start()

    ring = ((kbuf, k_send, k_recv), (vbuf, v_send, v_recv))

    loads[2].wait()
    wout_t[...] = wout[...].astype(F32).T.astype(BF16)
    wcol_t[head] = wout_t[pl.ds(pl.multiple_of(head * cols, cols), cols), :]

    def w_copy(step):
        other = (head + step) % n_head
        return remote(
            wout_t.at[pl.ds(pl.multiple_of(other * cols, cols), cols), :],
            wcol_t.at[head],
            w_send.at[step],
            w_recv.at[head],
            (ctx, other),
        )

    m_ref[...] = jnp.full_like(m_ref, -1e30)
    l_ref[...] = jnp.zeros_like(l_ref)
    acc[...] = jnp.zeros_like(acc)
    for step in range(1, 4):
        other = (mine + step) % 4
        remote(
            q_raw.at[other], q_raw.at[other], q_send.at[step], q_recv.at[other], dev_up
        ).wait_recv()
    low = lax.broadcasted_iota(jnp.int32, (rows, cols), 1) < HD
    for b in range(4):
        q = q_raw[b]
        zero = jnp.zeros_like(q)
        q_pad[0, b * rows : (b + 1) * rows, :] = jnp.where(low, q, zero)
        q_pad[1, b * rows : (b + 1) * rows, :] = jnp.where(low, zero, q)

    def attend(items, h, part):
        span = slice(part * 2 * rows, (part + 1) * 2 * rows)
        queries = q_pad[h, span, :]
        scores = [nt(kbuf[j], queries) for j in items]
        old = m_ref[h : h + 1, span]
        new = old
        for block in scores:
            new = jnp.maximum(new, jnp.max(block, axis=0, keepdims=True))
        weights = [jnp.exp2(block - new) for block in scores]
        shrink = jnp.exp2(old - new)
        m_ref[h : h + 1, span] = new
        total = l_ref[h : h + 1, span] * shrink
        summed = acc[h, :, span] * shrink
        for j, block in zip(items, weights):
            total = total + jnp.sum(block, axis=0, keepdims=True)
            summed = summed + nn(vbuf[j, h * HD : (h + 1) * HD, :], block.astype(BF16))
        l_ref[h : h + 1, span] = total
        acc[h, :, span] = summed

    for i in range(4):
        arrive(1 + i // 2, *ring[i % 2])
        attend((0,), i // 2, i % 2)
    w_copy(last).start()

    @pl.loop(1, nz // 2)
    def _(hop):
        first_item = 2 * hop - 1
        w_copy(first_item).start()
        w_copy(first_item + 1).start()
        for i in range(4):
            j = first_item + 2 + i // 2

            @pl.when(j <= last)
            def _():
                arrive(j, *ring[i % 2])

            attend((first_item, first_item + 1), i // 2, i % 2)

    for i in range(4):
        attend((last,), i // 2, i % 2)

    c_copies = []
    for step in (2, 1, 3):
        other = (mine + step) % 4
        span = pl.ds(pl.multiple_of(other * rows, rows), rows)
        for h in range(2):
            part_send[other, h * HD : (h + 1) * HD, :] = acc[h, :, span].astype(BF16)
            stat_send[other, h : h + 1, :] = m_ref[h : h + 1, span]
            stat_send[other, 2 + h : 3 + h, :] = l_ref[h : h + 1, span]
        device = (z * 4 + other, head)
        c_copies.append(
            remote(part_send.at[other], part_recv.at[mine], c_send.at[step], c_recv.at[mine], device)
        )
        c_copies.append(
            remote(
                stat_send.at[other], stat_recv.at[mine], st_send.at[step], st_recv.at[mine], device
            )
        )
        c_copies[-2].start()
        c_copies[-1].start()

    @pl.loop(1, last)
    def _(j):
        @pl.when(passes_on(j))
        def _():
            forward(j, kbuf, k_send, k_recv).wait_send()
            forward(j, vbuf, v_send, v_recv).wait_send()

    for copy in first + q_copies:
        copy.wait_send()

    for step in range(1, 4):
        other = (mine + step) % 4
        remote(
            part_recv.at[other], part_recv.at[other], c_send.at[step], c_recv.at[other], dev_up
        ).wait_recv()
        remote(
            stat_recv.at[other], stat_recv.at[other], st_send.at[step], st_recv.at[other], dev_up
        ).wait_recv()
    span = pl.ds(pl.multiple_of(mine * rows, rows), rows)
    for h in range(2):
        tops = [m_ref[h : h + 1, span]]
        sums = [l_ref[h : h + 1, span]]
        parts = [acc[h, :, span]]
        for step in range(1, 4):
            other = (mine + step) % 4
            tops.append(stat_recv[other, h : h + 1, :])
            sums.append(stat_recv[other, 2 + h : 3 + h, :])
            parts.append(part_recv[other, h * HD : (h + 1) * HD, :].astype(F32))
        top = functools.reduce(jnp.maximum, tops)
        scales = [jnp.exp2(t - top) for t in tops]
        total = functools.reduce(jnp.add, [a * b for a, b in zip(scales, sums)])
        inverse = 1.0 / total
        mixed = functools.reduce(jnp.add, [(a * inverse) * b for a, b in zip(scales, parts)])
        att[head, h * HD : (h + 1) * HD, :] = mixed.astype(BF16)

    sign = 1 - 2 * core

    def along(side, steps):
        return side * ny + (y + sign * steps + ny) % ny

    other_side = 1 - xl
    pair = (ctx, along(other_side, 0))
    pos, pos2 = (ctx, along(xl, 1)), (ctx, along(xl, 2))
    neg, neg2 = (ctx, along(xl, -1)), (ctx, along(xl, -2))

    def gather(which, buf, use):
        started = []

        def send(src, *routes):
            for sems, device in routes:
                copy = remote(
                    buf.at[src], buf.at[src], sems.at[which, src], g_recv.at[which, src], device
                )
                copy.start()
                started.append(copy)

        def wait(src):
            remote(
                buf.at[src], buf.at[src], g_pos.at[which, src], g_recv.at[which, src], pos
            ).wait_recv()

        to_pair = (g_pair, pair)
        to_pos, to_pos2 = (g_pos, pos), (g_pos2, pos2)
        to_neg, to_neg2 = (g_neg, neg), (g_neg2, neg2)
        send(head, to_pair, to_pos2, to_neg2, to_pos, to_neg)
        mate = along(other_side, 0)
        ahead = [along(xl, d) for d in range(1, 5)]
        behind = [along(xl, -d) for d in range(1, 4)]
        far_ahead = [along(other_side, d) for d in range(1, 5)]
        far_behind = [along(other_side, -d) for d in range(1, 4)]
        use(head)
        wait(mate)
        send(mate, to_pos2, to_pos)
        wait(ahead[0])
        send(ahead[0], to_pair)
        wait(ahead[1])
        send(ahead[1], to_neg2, to_neg, to_pair)
        wait(behind[0])
        wait(behind[1])
        send(behind[1], to_pos)
        for src in (mate, ahead[0], ahead[1], behind[0], behind[1]):
            use(src)
        wait(far_behind[1])
        send(far_behind[1], to_pos)
        wait(ahead[2])
        send(ahead[2], to_pair)
        wait(ahead[3])
        send(ahead[3], to_pair)
        for src in (far_behind[1], ahead[2], ahead[3]):
            use(src)
        for src in (far_behind[0], far_ahead[0], behind[2], far_ahead[1]):
            wait(src)
            use(src)
        for src in (far_behind[2], far_ahead[2], far_ahead[3]):
            wait(src)
            use(src)
        return started

    residual = tok[:, pl.ds(pl.multiple_of(head * cols, cols), cols)].astype(F32).T

    @pl.loop(1, n_head)
    def _(step):
        other = (head + step) % n_head
        remote(
            wcol_t.at[other], wcol_t.at[other], w_send.at[step], w_recv.at[other], pos
        ).wait_recv()

    total = [residual]

    def project(src):
        total[0] = total[0] + nn(wcol_t[src], att[src])

    started = gather(0, att, project)
    hid[head] = total[0].astype(BF16)

    ext = [jnp.zeros((wdec.shape[0], rows), F32)]
    squares = [jnp.zeros((cols, rows), F32)]

    def decode(src):
        block = hid[src]
        wide = block.astype(F32)
        squares[0] = squares[0] + wide * wide
        ext[0] = ext[0] + nn(wdec[:, pl.ds(pl.multiple_of(src * cols, cols), cols)], block)

    loads[3].wait()
    started += gather(1, hid, decode)
    mean = jnp.sum(squares[0], axis=0, keepdims=True) * (1.0 / width)
    field = ext[0] * lax.rsqrt(mean + EPS)

    edge = OV * 16
    halo_send[0] = field[cells + edge :, :].astype(BF16)
    halo_send[1] = field[:edge, :].astype(BF16)
    halos = []
    for i, device in enumerate((((ctx + 1) % n_ctx, head), ((ctx + n_ctx - 1) % n_ctx, head))):
        halos.append(
            remote(halo_send.at[i], halo_recv.at[i], halo_ssem.at[i], halo_rsem.at[i], device)
        )
    for copy in halos:
        copy.start()
    out_ref[edge : cells - edge, :] = field[2 * edge : cells, :]
    for copy in started + c_copies:
        copy.wait_send()

    @pl.loop(1, n_head)
    def _(step):
        w_copy(step).wait_send()

    halos[0].wait()
    out_ref[:edge, :] = field[edge : 2 * edge, :] + halo_recv[0].astype(F32)
    halos[1].wait()
    out_ref[cells - edge :, :] = field[cells : cells + edge, :] + halo_recv[1].astype(F32)


def body(n_ctx, n_head, tokens, w_qkv, w_out, w_dec):
    rows, width = tokens.shape
    cols = w_qkv.shape[2]
    nz = n_ctx // 4
    wdec_t = jnp.transpose(w_dec, (1, 2, 0)).reshape(-1, width)
    cells = PATCH * w_dec.shape[2]
    dma = pltpu.SemaphoreType.DMA
    anywhere = pl.BlockSpec(memory_space=pl.ANY)
    flops = 2 * rows * width * (3 * cols + cols + wdec_t.shape[0])
    flops += 4 * (4 * rows) * (rows * nz) * cols
    out = pl.pallas_call(
        functools.partial(kernel, n_ctx, n_head),
        out_shape=jax.ShapeDtypeStruct((cells, rows), F32),
        in_specs=[anywhere] * 4,
        out_specs=pl.BlockSpec(memory_space=pltpu.VMEM),
        scratch_shapes=[
            pltpu.VMEM((rows, width), BF16),
            pltpu.VMEM(w_qkv.shape, BF16),
            pltpu.VMEM(w_out.shape, BF16),
            pltpu.VMEM(wdec_t.shape, BF16),
            pltpu.VMEM((width, cols), BF16),
            pltpu.VMEM((n_head, cols, cols), BF16),
            pltpu.VMEM((4, rows, cols), BF16),
            pltpu.VMEM((2, 4 * rows, cols), BF16),
            pltpu.VMEM((nz, rows, cols), BF16),
            pltpu.VMEM((nz, cols, rows), BF16),
            pltpu.VMEM((2, 4 * rows), F32),
            pltpu.VMEM((2, 4 * rows), F32),
            pltpu.VMEM((2, HD, 4 * rows), F32),
            pltpu.VMEM((4, cols, rows), BF16),
            pltpu.VMEM((4, 8, rows), F32),
            pltpu.VMEM((4, cols, rows), BF16),
            pltpu.VMEM((4, 8, rows), F32),
            pltpu.VMEM((n_head, cols, rows), BF16),
            pltpu.VMEM((n_head, cols, rows), BF16),
            pltpu.VMEM((2, 2 * OV * 8, rows), BF16),
            pltpu.VMEM((2, 2 * OV * 8, rows), BF16),
            dma((4,)),
            dma((4,)),
            dma((nz,)),
            dma((nz,)),
            dma((nz,)),
            dma((nz,)),
            dma((4,)),
            dma((4,)),
            dma((n_head,)),
            dma((n_head,)),
            dma((4,)),
            dma((4,)),
            dma((4,)),
            dma((4,)),
            dma((2, n_head)),
            dma((2, n_head)),
            dma((2, n_head)),
            dma((2, n_head)),
            dma((2, n_head)),
            dma((2, n_head)),
            dma((2,)),
            dma((2,)),
        ],
        compiler_params=pltpu.CompilerParams(
            collective_id=0, has_side_effects=True, vmem_limit_bytes=48 * 1024 * 1024
        ),
        cost_estimate=pl.CostEstimate(flops=flops, bytes_accessed=1 << 22, transcendentals=1 << 23),
        name="layer",
    )(tokens, w_qkv, w_out, wdec_t)
    return jnp.transpose(out.reshape(PATCH, w_dec.shape[2], rows), (2, 0, 1))


def solution(mesh):
    return jax.shard_map(
        functools.partial(body, mesh.shape["ctx"], mesh.shape["head"]),
        mesh=mesh,
        in_specs=(P("ctx", None), P(None, None, "head"), P("head", None), P(None, None, "head")),
        out_specs=P("ctx", None, "head"),
        check_vma=False,
    )
```

```python
import functools

import jax
import jax.numpy as jnp
from jax import lax
from jax.experimental import pallas as pl
from jax.experimental.pallas import tpu as pltpu
from jax.sharding import PartitionSpec as P

HD = 64
PATCH = 8
OV = 2
EPS = 1e-05
LOG2E = 1.4426950408889634
F32 = jnp.float32
BF16 = jnp.bfloat16


def nt(a, b):
    return lax.dot_general(a, b, (((1,), (1,)), ((), ())), preferred_element_type=F32)


def tn(a, b):
    return lax.dot_general(a, b, (((0,), (0,)), ((), ())), preferred_element_type=F32)


def nn(a, b):
    return jnp.dot(a, b, preferred_element_type=F32)


def kernel(
    n_ctx,
    n_head,
    tok_hbm,
    wqkv_hbm,
    wout_hbm,
    wdec_hbm,
    out_ref,
    tok,
    wqkv,
    wdec,
    wcol,
    q_raw,
    q_pad,
    kbuf,
    vbuf,
    m_ref,
    l_ref,
    acc,
    part_send,
    stat_send,
    part_recv,
    stat_recv,
    att,
    hid,
    halo_send,
    halo_recv,
    load_sem,
    own_send,
    k_send,
    v_send,
    k_recv,
    v_recv,
    q_send,
    q_recv,
    w_send,
    w_recv,
    c_send,
    c_recv,
    st_send,
    st_recv,
    g_recv,
    g_pos,
    g_neg,
    g_pos2,
    g_neg2,
    g_pair,
    halo_ssem,
    halo_rsem,
):
    rows, width = tok.shape
    nz, ny = n_ctx // 4, n_head // 2
    last = nz - 1
    cols = 2 * HD
    cells = PATCH * 16

    ctx = lax.axis_index("ctx")
    head = lax.axis_index("head")
    core = ctx % 2
    xh = (ctx // 2) % 2
    z = ctx // 4
    xl = head // ny
    y = head % ny
    mine = xh * 2 + core
    up = (z + 1) % nz
    down = (z + nz - 1) % nz
    dev_up = (up * 4 + xh * 2, head)
    dev_down = (down * 4 + xh * 2 + 1, head)

    def remote(src, dst, ssem, rsem, device):
        return pltpu.make_async_remote_copy(
            src_ref=src,
            dst_ref=dst,
            send_sem=ssem,
            recv_sem=rsem,
            device_id=device,
            device_id_type=pl.DeviceIdType.MESH,
        )

    own_cols = pl.ds(pl.multiple_of(head * cols, cols), cols)
    loads = [
        pltpu.make_async_copy(a, b, load_sem.at[i])
        for i, (a, b) in enumerate(
            (
                (tok_hbm, tok),
                (wqkv_hbm, wqkv),
                (wout_hbm.at[:, own_cols], wcol.at[head]),
                (wdec_hbm, wdec),
            )
        )
    ]
    for load in loads:
        load.start()

    barrier = pltpu.get_barrier_semaphore()

    def greet(device):
        pl.semaphore_signal(
            barrier, inc=1, device_id=device, device_id_type=pl.DeviceIdType.MESH
        )

    source_z = (z + nz - 1 + 2 * core) % nz
    greet((source_z * 4 + xh * 2, head))
    greet((source_z * 4 + xh * 2 + 1, head))
    for step in range(1, 4):
        other = (mine + step) % 4
        greet((z * 4 + other, head))

    @pl.loop(1, n_head)
    def _(step):
        greet((ctx, (head + step) % n_head))

    greet(((ctx + 1) % n_ctx, head))
    greet(((ctx + n_ctx - 1) % n_ctx, head))

    pl.semaphore_wait(barrier, n_head + 6)

    def w_copy(step):
        other = (head + step) % n_head
        return remote(
            wout_hbm.at[:, pl.ds(pl.multiple_of(other * cols, cols), cols)],
            wcol.at[head],
            w_send.at[step],
            w_recv.at[head],
            (ctx, other),
        )

    loads[0].wait()
    loads[1].wait()
    x = tok[...]
    xf = x.astype(F32)
    r = lax.rsqrt(jnp.mean(xf * xf, axis=-1, keepdims=True) + EPS)
    keyvals = nn(x, jnp.concatenate([wqkv[1], wqkv[2]], axis=1)) * r
    kbuf[0] = keyvals[:, :cols].astype(BF16)
    vbuf[0] = keyvals[:, cols:].T.astype(BF16)

    first = []
    for t, device in enumerate((dev_up, dev_down)):
        first.append(
            remote(kbuf.at[0], kbuf.at[1 + core], own_send.at[2 * t], k_recv.at[1 + core], device)
        )
        first.append(
            remote(
                vbuf.at[0], vbuf.at[1 + core], own_send.at[2 * t + 1], v_recv.at[1 + core], device
            )
        )
    for copy in first:
        copy.start()

    q_raw[mine] = (nn(x, wqkv[0]) * (r * (HD**-0.5 * LOG2E))).astype(BF16)
    q_copies = []
    for step in (2, 1, 3):
        other = (mine + step) % 4
        q_copies.append(
            remote(
                q_raw.at[mine], q_raw.at[mine], q_send.at[step], q_recv.at[mine], (z * 4 + other, head)
            )
        )
    for copy in q_copies:
        copy.start()

    def forward(j, buf, ssem, rsem):
        target = jnp.minimum(j + 2, last)
        return remote(
            buf.at[j],
            buf.at[target],
            ssem.at[j],
            rsem.at[target],
            ((z + 1 + core * (nz - 2)) % nz * 4 + xh * 2 + core, head),
        )

    def passes_on(j):
        return jnp.logical_or(j <= last - 3, j == last - 2 + core)

    def arrive(j, buf, ssem, rsem):
        remote(buf.at[j], buf.at[j], ssem.at[j], rsem.at[j], dev_up).wait_recv()

        @pl.when(passes_on(j))
        def _():
            forward(j, buf, ssem, rsem).start()

    ring = ((kbuf, k_send, k_recv), (vbuf, v_send, v_recv))

    m_ref[...] = jnp.full_like(m_ref, -1e30)
    l_ref[...] = jnp.zeros_like(l_ref)
    acc[...] = jnp.zeros_like(acc)
    for step in range(1, 4):
        other = (mine + step) % 4
        remote(
            q_raw.at[other], q_raw.at[other], q_send.at[step], q_recv.at[other], dev_up
        ).wait_recv()
    low = lax.broadcasted_iota(jnp.int32, (rows, cols), 1) < HD
    for b in range(4):
        q = q_raw[b]
        zero = jnp.zeros_like(q)
        q_pad[0, b * rows : (b + 1) * rows, :] = jnp.where(low, q, zero)
        q_pad[1, b * rows : (b + 1) * rows, :] = jnp.where(low, zero, q)

    def attend(items, h, part):
        span = pl.ds(pl.multiple_of(part * 2 * rows, 2 * rows), 2 * rows)
        queries = q_pad[h, span, :]
        scores = [nt(kbuf[j], queries) for j in items]
        old = m_ref[h : h + 1, span]
        new = old
        for block in scores:
            new = jnp.maximum(new, jnp.max(block, axis=0, keepdims=True))
        weights = [jnp.exp2(block - new) for block in scores]
        shrink = jnp.exp2(old - new)
        m_ref[h : h + 1, span] = new
        total = l_ref[h : h + 1, span] * shrink
        summed = acc[h, :, span] * shrink
        for j, block in zip(items, weights):
            total = total + jnp.sum(block, axis=0, keepdims=True)
            summed = summed + nn(vbuf[j, h * HD : (h + 1) * HD, :], block.astype(BF16))
        l_ref[h : h + 1, span] = total
        acc[h, :, span] = summed

    for i in range(4):
        arrive(1 + i // 2, *ring[i % 2])
        attend((0,), i // 2, i % 2)

    w_copy(last).start()

    @pl.loop(1, nz // 2)
    def _(hop):
        first_item = 2 * hop - 1
        w_copy(first_item).start()
        w_copy(first_item + 1).start()
        for i in range(4):
            j = first_item + 2 + i // 2

            @pl.when(j <= last)
            def _():
                arrive(j, *ring[i % 2])

            attend((first_item, first_item + 1), i // 2, i % 2)

    c_copies = []

    def hand_over(step):
        other = (mine + step) % 4
        span = pl.ds(pl.multiple_of(other * rows, rows), rows)
        for h in range(2):
            part_send[other, h * HD : (h + 1) * HD, :] = acc[h, :, span].astype(BF16)
            stat_send[other, h : h + 1, :] = m_ref[h : h + 1, span]
            stat_send[other, 2 + h : 3 + h, :] = l_ref[h : h + 1, span]
        device = (z * 4 + other, head)
        for src, dst, ssem, rsem in (
            (part_send, part_recv, c_send, c_recv),
            (stat_send, stat_recv, st_send, st_recv),
        ):
            copy = remote(src.at[other], dst.at[mine], ssem.at[step], rsem.at[mine], device)
            copy.start()
            c_copies.append(copy)

    attend((last,), 0, 1 - xh)
    attend((last,), 1, 1 - xh)
    far_core = 3 - 2 * core
    near_core = 1 + 2 * core
    hand_over(2)
    hand_over(far_core)
    attend((last,), 0, xh)
    attend((last,), 1, xh)
    hand_over(near_core)

    @pl.loop(1, last)
    def _(j):
        @pl.when(passes_on(j))
        def _():
            forward(j, kbuf, k_send, k_recv).wait_send()
            forward(j, vbuf, v_send, v_recv).wait_send()

    for copy in first + q_copies:
        copy.wait_send()

    for step in range(1, 4):
        other = (mine + step) % 4
        remote(
            part_recv.at[other], part_recv.at[other], c_send.at[step], c_recv.at[other], dev_up
        ).wait_recv()
        remote(
            stat_recv.at[other], stat_recv.at[other], st_send.at[step], st_recv.at[other], dev_up
        ).wait_recv()
    span = pl.ds(pl.multiple_of(mine * rows, rows), rows)
    for h in range(2):
        tops = [m_ref[h : h + 1, span]]
        sums = [l_ref[h : h + 1, span]]
        parts = [acc[h, :, span]]
        for step in range(1, 4):
            other = (mine + step) % 4
            tops.append(stat_recv[other, h : h + 1, :])
            sums.append(stat_recv[other, 2 + h : 3 + h, :])
            parts.append(part_recv[other, h * HD : (h + 1) * HD, :].astype(F32))
        top = functools.reduce(jnp.maximum, tops)
        scales = [jnp.exp2(t - top) for t in tops]
        total = functools.reduce(jnp.add, [a * b for a, b in zip(scales, sums)])
        inverse = 1.0 / total
        mixed = functools.reduce(jnp.add, [(a * inverse) * b for a, b in zip(scales, parts)])
        att[head, h * HD : (h + 1) * HD, :] = mixed.astype(BF16)

    sign = 1 - 2 * core

    def along(side, steps):
        return side * ny + (y + sign * steps + ny) % ny

    other_side = 1 - xl
    pair = (ctx, along(other_side, 0))
    pos, pos2 = (ctx, along(xl, 1)), (ctx, along(xl, 2))
    neg, neg2 = (ctx, along(xl, -1)), (ctx, along(xl, -2))

    def gather(which, buf, use):
        started = []

        def send(src, *routes):
            for sems, device in routes:
                copy = remote(
                    buf.at[src], buf.at[src], sems.at[which, src], g_recv.at[which, src], device
                )
                copy.start()
                started.append(copy)

        def wait(src):
            remote(
                buf.at[src], buf.at[src], g_pos.at[which, src], g_recv.at[which, src], pos
            ).wait_recv()

        to_pair = (g_pair, pair)
        to_pos, to_pos2 = (g_pos, pos), (g_pos2, pos2)
        to_neg, to_neg2 = (g_neg, neg), (g_neg2, neg2)
        send(head, to_pair, to_pos2, to_neg2, to_pos, to_neg)
        mate = along(other_side, 0)
        ahead = [along(xl, d) for d in range(1, 5)]
        behind = [along(xl, -d) for d in range(1, 4)]
        far_ahead = [along(other_side, d) for d in range(1, 5)]
        far_behind = [along(other_side, -d) for d in range(1, 4)]
        use(head)
        wait(mate)
        send(mate, to_pos2, to_pos)
        wait(behind[0])
        wait(ahead[0])
        send(ahead[0], to_pair)
        wait(ahead[1])
        send(ahead[1], to_neg2, to_neg, to_pair)
        for src in (mate, ahead[0], ahead[1], behind[0]):
            use(src)
        wait(behind[1])
        send(behind[1], to_pos)
        use(behind[1])
        wait(far_behind[1])
        send(far_behind[1], to_pos)
        wait(ahead[2])
        send(ahead[2], to_pair)
        wait(ahead[3])
        send(ahead[3], to_pair)
        for src in (far_behind[1], ahead[2], ahead[3]):
            use(src)
        for src in (far_behind[0], far_ahead[0], behind[2], far_ahead[1]):
            wait(src)
            use(src)
        for src in (far_behind[2], far_ahead[2], far_ahead[3]):
            wait(src)
            use(src)
        return started

    residual = tok[:, pl.ds(pl.multiple_of(head * cols, cols), cols)].astype(F32).T

    @pl.loop(1, n_head)
    def _(step):
        other = (head + step) % n_head
        remote(
            wcol.at[other], wcol.at[other], w_send.at[step], w_recv.at[other], pos
        ).wait_recv()

    loads[2].wait()
    total = [residual]

    def project(src):
        total[0] = total[0] + tn(wcol[src], att[src])

    started = gather(0, att, project)
    hid[head] = total[0].astype(BF16)

    ext = [jnp.zeros((wdec.shape[0], rows), F32)]
    squares = [jnp.zeros((cols, rows), F32)]

    def decode(src):
        block = hid[src]
        wide = block.astype(F32)
        squares[0] = squares[0] + wide * wide
        ext[0] = ext[0] + nn(wdec[:, pl.ds(pl.multiple_of(src * cols, cols), cols)], block)

    loads[3].wait()
    started += gather(1, hid, decode)
    mean = jnp.sum(squares[0], axis=0, keepdims=True) * (1.0 / width)
    field = ext[0] * lax.rsqrt(mean + EPS)

    edge = OV * 16
    halo_send[0] = field[cells + edge :, :].astype(BF16)
    halo_send[1] = field[:edge, :].astype(BF16)
    halos = []
    for i, device in enumerate((((ctx + 1) % n_ctx, head), ((ctx + n_ctx - 1) % n_ctx, head))):
        halos.append(
            remote(halo_send.at[i], halo_recv.at[i], halo_ssem.at[i], halo_rsem.at[i], device)
        )
    for copy in halos:
        copy.start()
    out_ref[edge : cells - edge, :] = field[2 * edge : cells, :]
    for copy in started + c_copies:
        copy.wait_send()

    @pl.loop(1, n_head)
    def _(step):
        w_copy(step).wait_send()

    halos[0].wait()
    out_ref[:edge, :] = field[edge : 2 * edge, :] + halo_recv[0].astype(F32)
    halos[1].wait()
    out_ref[cells - edge :, :] = field[cells : cells + edge, :] + halo_recv[1].astype(F32)


def body(n_ctx, n_head, tokens, w_qkv, w_out, w_dec):
    rows, width = tokens.shape
    cols = w_qkv.shape[2]
    nz = n_ctx // 4
    wdec_t = jnp.transpose(w_dec, (1, 2, 0)).reshape(-1, width)
    cells = PATCH * w_dec.shape[2]
    dma = pltpu.SemaphoreType.DMA
    anywhere = pl.BlockSpec(memory_space=pl.ANY)
    flops = 2 * rows * width * (3 * cols + cols + wdec_t.shape[0])
    flops += 4 * (4 * rows) * (rows * nz) * cols
    out = pl.pallas_call(
        functools.partial(kernel, n_ctx, n_head),
        out_shape=jax.ShapeDtypeStruct((cells, rows), F32),
        in_specs=[anywhere] * 4,
        out_specs=pl.BlockSpec(memory_space=pltpu.VMEM),
        scratch_shapes=[
            pltpu.VMEM((rows, width), BF16),
            pltpu.VMEM(w_qkv.shape, BF16),
            pltpu.VMEM(wdec_t.shape, BF16),
            pltpu.VMEM((n_head, cols, cols), BF16),
            pltpu.VMEM((4, rows, cols), BF16),
            pltpu.VMEM((2, 4 * rows, cols), BF16),
            pltpu.VMEM((nz, rows, cols), BF16),
            pltpu.VMEM((nz, cols, rows), BF16),
            pltpu.VMEM((2, 4 * rows), F32),
            pltpu.VMEM((2, 4 * rows), F32),
            pltpu.VMEM((2, HD, 4 * rows), F32),
            pltpu.VMEM((4, cols, rows), BF16),
            pltpu.VMEM((4, 8, rows), F32),
            pltpu.VMEM((4, cols, rows), BF16),
            pltpu.VMEM((4, 8, rows), F32),
            pltpu.VMEM((n_head, cols, rows), BF16),
            pltpu.VMEM((n_head, cols, rows), BF16),
            pltpu.VMEM((2, 2 * OV * 8, rows), BF16),
            pltpu.VMEM((2, 2 * OV * 8, rows), BF16),
            dma((4,)),
            dma((4,)),
            dma((nz,)),
            dma((nz,)),
            dma((nz,)),
            dma((nz,)),
            dma((4,)),
            dma((4,)),
            dma((n_head,)),
            dma((n_head,)),
            dma((4,)),
            dma((4,)),
            dma((4,)),
            dma((4,)),
            dma((2, n_head)),
            dma((2, n_head)),
            dma((2, n_head)),
            dma((2, n_head)),
            dma((2, n_head)),
            dma((2, n_head)),
            dma((2,)),
            dma((2,)),
        ],
        compiler_params=pltpu.CompilerParams(
            collective_id=0, has_side_effects=True, vmem_limit_bytes=60 * 1024 * 1024
        ),
        cost_estimate=pl.CostEstimate(flops=flops, bytes_accessed=1 << 22, transcendentals=1 << 23),
        name="layer",
    )(tokens, w_qkv, w_out, wdec_t)
    return jnp.transpose(out.reshape(PATCH, w_dec.shape[2], rows), (2, 0, 1))


def solution(mesh):
    return jax.shard_map(
        functools.partial(body, mesh.shape["ctx"], mesh.shape["head"]),
        mesh=mesh,
        in_specs=(P("ctx", None), P(None, None, "head"), P("head", None), P(None, None, "head")),
        out_specs=P("ctx", None, "head"),
        check_vma=False,
    )
```

```python
import functools

import jax
import jax.numpy as jnp
from jax import lax
from jax.experimental import pallas as pl
from jax.experimental.pallas import tpu as pltpu
from jax.sharding import PartitionSpec as P

HD = 64
PATCH = 8
OV = 2
EPS = 1e-05
LOG2E = 1.4426950408889634
F32 = jnp.float32
BF16 = jnp.bfloat16


def nt(a, b):
    return lax.dot_general(a, b, (((1,), (1,)), ((), ())), preferred_element_type=F32)


def tn(a, b):
    return lax.dot_general(a, b, (((0,), (0,)), ((), ())), preferred_element_type=F32)


def nn(a, b):
    return jnp.dot(a, b, preferred_element_type=F32)


def kernel(
    n_ctx,
    n_head,
    tok_hbm,
    wqkv_hbm,
    wout_hbm,
    wdec_hbm,
    out_ref,
    tok,
    wqkv,
    wdec,
    wcol,
    q_raw,
    q_pad,
    kbuf,
    vbuf,
    m_ref,
    l_ref,
    acc,
    part_send,
    stat_send,
    part_recv,
    stat_recv,
    att,
    hid,
    halo_send,
    halo_recv,
    load_sem,
    own_send,
    k_send,
    v_send,
    k_recv,
    v_recv,
    q_send,
    q_recv,
    w_send,
    w_recv,
    c_send,
    c_recv,
    st_send,
    st_recv,
    g_recv,
    g_pos,
    g_neg,
    g_pos2,
    g_neg2,
    g_pair,
    halo_ssem,
    halo_rsem,
):
    rows, width = tok.shape
    nz, ny = n_ctx // 4, n_head // 2
    last = nz - 1
    cols = 2 * HD
    cells = PATCH * 16

    ctx = lax.axis_index("ctx")
    head = lax.axis_index("head")
    core = ctx % 2
    xh = (ctx // 2) % 2
    z = ctx // 4
    xl = head // ny
    y = head % ny
    mine = xh * 2 + core
    up = (z + 1) % nz
    down = (z + nz - 1) % nz
    dev_up = (up * 4 + xh * 2, head)
    dev_down = (down * 4 + xh * 2 + 1, head)

    def remote(src, dst, ssem, rsem, device):
        return pltpu.make_async_remote_copy(
            src_ref=src,
            dst_ref=dst,
            send_sem=ssem,
            recv_sem=rsem,
            device_id=device,
            device_id_type=pl.DeviceIdType.MESH,
        )

    own_cols = pl.ds(pl.multiple_of(head * cols, cols), cols)
    loads = [
        pltpu.make_async_copy(a, b, load_sem.at[i])
        for i, (a, b) in enumerate(
            (
                (tok_hbm, tok),
                (wqkv_hbm, wqkv),
                (wout_hbm.at[:, own_cols], wcol.at[head]),
                (wdec_hbm, wdec),
            )
        )
    ]
    for load in loads:
        load.start()

    barrier = pltpu.get_barrier_semaphore()

    def greet(device):
        pl.semaphore_signal(
            barrier, inc=1, device_id=device, device_id_type=pl.DeviceIdType.MESH
        )

    source_z = (z + nz - 1 + 2 * core) % nz
    greet((source_z * 4 + xh * 2, head))
    greet((source_z * 4 + xh * 2 + 1, head))
    for step in range(1, 4):
        other = (mine + step) % 4
        greet((z * 4 + other, head))

    @pl.loop(1, n_head)
    def _(step):
        greet((ctx, (head + step) % n_head))

    greet(((ctx + 1) % n_ctx, head))
    greet(((ctx + n_ctx - 1) % n_ctx, head))

    pl.semaphore_wait(barrier, n_head + 6)

    def w_copy(step):
        other = (head + step) % n_head
        return remote(
            wout_hbm.at[:, pl.ds(pl.multiple_of(other * cols, cols), cols)],
            wcol.at[head],
            w_send.at[step],
            w_recv.at[head],
            (ctx, other),
        )

    loads[0].wait()
    loads[1].wait()
    x = tok[...]
    xf = x.astype(F32)
    r = lax.rsqrt(jnp.mean(xf * xf, axis=-1, keepdims=True) + EPS)
    keyvals = nn(x, jnp.concatenate([wqkv[1], wqkv[2]], axis=1)) * r
    kbuf[0] = keyvals[:, :cols].astype(BF16)
    vbuf[0] = keyvals[:, cols:].T.astype(BF16)

    first = []
    for t, device in enumerate((dev_up, dev_down)):
        first.append(
            remote(kbuf.at[0], kbuf.at[1 + core], own_send.at[2 * t], k_recv.at[1 + core], device)
        )
        first.append(
            remote(
                vbuf.at[0], vbuf.at[1 + core], own_send.at[2 * t + 1], v_recv.at[1 + core], device
            )
        )
    for copy in first:
        copy.start()

    q_raw[mine] = (nn(x, wqkv[0]) * (r * (HD**-0.5 * LOG2E))).astype(BF16)
    q_copies = []
    for step in (2, 1, 3):
        other = (mine + step) % 4
        q_copies.append(
            remote(
                q_raw.at[mine], q_raw.at[mine], q_send.at[step], q_recv.at[mine], (z * 4 + other, head)
            )
        )
    for copy in q_copies:
        copy.start()

    def forward(j, buf, ssem, rsem):
        target = jnp.minimum(j + 2, last)
        return remote(
            buf.at[j],
            buf.at[target],
            ssem.at[j],
            rsem.at[target],
            ((z + 1 + core * (nz - 2)) % nz * 4 + xh * 2 + core, head),
        )

    def passes_on(j):
        return jnp.logical_or(j <= last - 3, j == last - 2 + core)

    def arrive(j, buf, ssem, rsem):
        remote(buf.at[j], buf.at[j], ssem.at[j], rsem.at[j], dev_up).wait_recv()

        @pl.when(passes_on(j))
        def _():
            forward(j, buf, ssem, rsem).start()

    ring = ((kbuf, k_send, k_recv), (vbuf, v_send, v_recv))

    m_ref[...] = jnp.full_like(m_ref, -1e30)
    l_ref[...] = jnp.zeros_like(l_ref)
    acc[...] = jnp.zeros_like(acc)
    far_core = 3 - 2 * core
    near_core = 1 + 2 * core
    low = lax.broadcasted_iota(jnp.int32, (rows, cols), 1) < HD

    def queries_from(step):
        other = (mine + step) % 4
        remote(
            q_raw.at[other], q_raw.at[other], q_send.at[step], q_recv.at[other], dev_up
        ).wait_recv()

    def spread_queries(part):
        for c in range(2):
            b = part * 2 + c
            q = q_raw[b]
            zero = jnp.zeros_like(q)
            place = pl.ds(pl.multiple_of(b * rows, rows), rows)
            q_pad[0, place, :] = jnp.where(low, q, zero)
            q_pad[1, place, :] = jnp.where(low, zero, q)

    def attend(items, h, part):
        if part is None:
            span = slice(0, 4 * rows)
        else:
            span = pl.ds(pl.multiple_of(part * 2 * rows, 2 * rows), 2 * rows)
        queries = q_pad[h, span, :]
        scores = [nt(kbuf[j], queries) for j in items]
        old = m_ref[h : h + 1, span]
        new = old
        for block in scores:
            new = jnp.maximum(new, jnp.max(block, axis=0, keepdims=True))
        weights = [jnp.exp2(block - new) for block in scores]
        shrink = jnp.exp2(old - new)
        m_ref[h : h + 1, span] = new
        total = l_ref[h : h + 1, span] * shrink
        summed = acc[h, :, span] * shrink
        for j, block in zip(items, weights):
            total = total + jnp.sum(block, axis=0, keepdims=True)
            summed = summed + nn(vbuf[j, h * HD : (h + 1) * HD, :], block.astype(BF16))
        l_ref[h : h + 1, span] = total
        acc[h, :, span] = summed

    queries_from(near_core)
    spread_queries(xh)
    for h in range(2):
        arrive(1, *ring[h])
        attend((0,), h, xh)
    for i in range(2):
        arrive(2, *ring[i])
    w_copy(1).start()
    for h in range(2):
        arrive(3, *ring[h])
        attend((1, 2), h, xh)
    for i in range(2):
        arrive(4, *ring[i])
    w_copy(2).start()
    queries_from(2)
    queries_from(far_core)
    spread_queries(1 - xh)
    for h in range(2):
        attend((0,), h, 1 - xh)
        arrive(5, *ring[h])
    for h in range(2):
        attend((1, 2), h, 1 - xh)
        arrive(6, *ring[h])
    w_copy(last).start()

    @pl.loop(2, nz // 2)
    def _(hop):
        first_item = 2 * hop - 1
        w_copy(first_item).start()
        w_copy(first_item + 1).start()
        for i in range(4):
            j = first_item + 4 + i // 2

            @pl.when(j <= last)
            def _():
                arrive(j, *ring[i % 2])

            if i % 2:
                attend((first_item, first_item + 1), i // 2, None)

    c_copies = []

    def hand_over(step):
        other = (mine + step) % 4
        span = pl.ds(pl.multiple_of(other * rows, rows), rows)
        for h in range(2):
            part_send[other, h * HD : (h + 1) * HD, :] = acc[h, :, span].astype(BF16)
            stat_send[other, h : h + 1, :] = m_ref[h : h + 1, span]
            stat_send[other, 2 + h : 3 + h, :] = l_ref[h : h + 1, span]
        device = (z * 4 + other, head)
        for src, dst, ssem, rsem in (
            (part_send, part_recv, c_send, c_recv),
            (stat_send, stat_recv, st_send, st_recv),
        ):
            copy = remote(src.at[other], dst.at[mine], ssem.at[step], rsem.at[mine], device)
            copy.start()
            c_copies.append(copy)

    attend((last,), 0, 1 - xh)
    attend((last,), 1, 1 - xh)
    hand_over(2)
    hand_over(far_core)
    attend((last,), 0, xh)
    attend((last,), 1, xh)
    hand_over(near_core)

    @pl.loop(1, last)
    def _(j):
        @pl.when(passes_on(j))
        def _():
            forward(j, kbuf, k_send, k_recv).wait_send()
            forward(j, vbuf, v_send, v_recv).wait_send()

    for copy in first + q_copies:
        copy.wait_send()

    for step in range(1, 4):
        other = (mine + step) % 4
        remote(
            part_recv.at[other], part_recv.at[other], c_send.at[step], c_recv.at[other], dev_up
        ).wait_recv()
        remote(
            stat_recv.at[other], stat_recv.at[other], st_send.at[step], st_recv.at[other], dev_up
        ).wait_recv()
    span = pl.ds(pl.multiple_of(mine * rows, rows), rows)
    for h in range(2):
        tops = [m_ref[h : h + 1, span]]
        sums = [l_ref[h : h + 1, span]]
        parts = [acc[h, :, span]]
        for step in range(1, 4):
            other = (mine + step) % 4
            tops.append(stat_recv[other, h : h + 1, :])
            sums.append(stat_recv[other, 2 + h : 3 + h, :])
            parts.append(part_recv[other, h * HD : (h + 1) * HD, :].astype(F32))
        top = functools.reduce(jnp.maximum, tops)
        scales = [jnp.exp2(t - top) for t in tops]
        total = functools.reduce(jnp.add, [a * b for a, b in zip(scales, sums)])
        inverse = 1.0 / total
        mixed = functools.reduce(jnp.add, [(a * inverse) * b for a, b in zip(scales, parts)])
        att[head, h * HD : (h + 1) * HD, :] = mixed.astype(BF16)

    sign = 1 - 2 * core

    def along(side, steps):
        return side * ny + (y + sign * steps + ny) % ny

    other_side = 1 - xl
    pair = (ctx, along(other_side, 0))
    pos, pos2 = (ctx, along(xl, 1)), (ctx, along(xl, 2))
    neg, neg2 = (ctx, along(xl, -1)), (ctx, along(xl, -2))

    def gather(which, buf, use):
        started = []

        def send(src, *routes):
            for sems, device in routes:
                copy = remote(
                    buf.at[src], buf.at[src], sems.at[which, src], g_recv.at[which, src], device
                )
                copy.start()
                started.append(copy)

        def wait(src):
            remote(
                buf.at[src], buf.at[src], g_pos.at[which, src], g_recv.at[which, src], pos
            ).wait_recv()

        to_pair = (g_pair, pair)
        to_pos, to_pos2 = (g_pos, pos), (g_pos2, pos2)
        to_neg, to_neg2 = (g_neg, neg), (g_neg2, neg2)
        send(head, to_pair, to_pos2, to_neg2, to_pos, to_neg)
        mate = along(other_side, 0)
        ahead = [along(xl, d) for d in range(1, 5)]
        behind = [along(xl, -d) for d in range(1, 4)]
        far_ahead = [along(other_side, d) for d in range(1, 5)]
        far_behind = [along(other_side, -d) for d in range(1, 4)]
        use(head)
        wait(mate)
        send(mate, to_pos2, to_pos)
        wait(behind[0])
        wait(ahead[0])
        send(ahead[0], to_pair)
        wait(ahead[1])
        send(ahead[1], to_neg2, to_neg, to_pair)
        for src in (mate, ahead[0], ahead[1], behind[0]):
            use(src)
        wait(behind[1])
        send(behind[1], to_pos)
        use(behind[1])
        wait(far_behind[1])
        send(far_behind[1], to_pos)
        wait(ahead[2])
        send(ahead[2], to_pair)
        wait(ahead[3])
        send(ahead[3], to_pair)
        for src in (far_behind[1], ahead[2], ahead[3]):
            use(src)
        for src in (far_behind[0], far_ahead[0], behind[2], far_ahead[1]):
            wait(src)
            use(src)
        for src in (far_behind[2], far_ahead[2], far_ahead[3]):
            wait(src)
            use(src)
        return started

    residual = tok[:, pl.ds(pl.multiple_of(head * cols, cols), cols)].astype(F32).T

    @pl.loop(1, n_head)
    def _(step):
        other = (head + step) % n_head
        remote(
            wcol.at[other], wcol.at[other], w_send.at[step], w_recv.at[other], pos
        ).wait_recv()

    loads[2].wait()
    total = [residual]

    def project(src):
        total[0] = total[0] + tn(wcol[src], att[src])

    started = gather(0, att, project)
    hid[head] = total[0].astype(BF16)

    ext = [jnp.zeros((wdec.shape[0], rows), F32)]
    squares = [jnp.zeros((cols, rows), F32)]

    def decode(src):
        block = hid[src]
        wide = block.astype(F32)
        squares[0] = squares[0] + wide * wide
        ext[0] = ext[0] + nn(wdec[:, pl.ds(pl.multiple_of(src * cols, cols), cols)], block)

    loads[3].wait()
    started += gather(1, hid, decode)
    mean = jnp.sum(squares[0], axis=0, keepdims=True) * (1.0 / width)
    field = ext[0] * lax.rsqrt(mean + EPS)

    edge = OV * 16
    halo_send[0] = field[cells + edge :, :].astype(BF16)
    halo_send[1] = field[:edge, :].astype(BF16)
    halos = []
    for i, device in enumerate((((ctx + 1) % n_ctx, head), ((ctx + n_ctx - 1) % n_ctx, head))):
        halos.append(
            remote(halo_send.at[i], halo_recv.at[i], halo_ssem.at[i], halo_rsem.at[i], device)
        )
    for copy in halos:
        copy.start()
    out_ref[edge : cells - edge, :] = field[2 * edge : cells, :]
    for copy in started + c_copies:
        copy.wait_send()

    @pl.loop(1, n_head)
    def _(step):
        w_copy(step).wait_send()

    halos[0].wait()
    out_ref[:edge, :] = field[edge : 2 * edge, :] + halo_recv[0].astype(F32)
    halos[1].wait()
    out_ref[cells - edge :, :] = field[cells : cells + edge, :] + halo_recv[1].astype(F32)


def body(n_ctx, n_head, tokens, w_qkv, w_out, w_dec):
    rows, width = tokens.shape
    cols = w_qkv.shape[2]
    nz = n_ctx // 4
    wdec_t = jnp.transpose(w_dec, (1, 2, 0)).reshape(-1, width)
    cells = PATCH * w_dec.shape[2]
    dma = pltpu.SemaphoreType.DMA
    anywhere = pl.BlockSpec(memory_space=pl.ANY)
    flops = 2 * rows * width * (3 * cols + cols + wdec_t.shape[0])
    flops += 4 * (4 * rows) * (rows * nz) * cols
    out = pl.pallas_call(
        functools.partial(kernel, n_ctx, n_head),
        out_shape=jax.ShapeDtypeStruct((cells, rows), F32),
        in_specs=[anywhere] * 4,
        out_specs=pl.BlockSpec(memory_space=pltpu.VMEM),
        scratch_shapes=[
            pltpu.VMEM((rows, width), BF16),
            pltpu.VMEM(w_qkv.shape, BF16),
            pltpu.VMEM(wdec_t.shape, BF16),
            pltpu.VMEM((n_head, cols, cols), BF16),
            pltpu.VMEM((4, rows, cols), BF16),
            pltpu.VMEM((2, 4 * rows, cols), BF16),
            pltpu.VMEM((nz, rows, cols), BF16),
            pltpu.VMEM((nz, cols, rows), BF16),
            pltpu.VMEM((2, 4 * rows), F32),
            pltpu.VMEM((2, 4 * rows), F32),
            pltpu.VMEM((2, HD, 4 * rows), F32),
            pltpu.VMEM((4, cols, rows), BF16),
            pltpu.VMEM((4, 8, rows), F32),
            pltpu.VMEM((4, cols, rows), BF16),
            pltpu.VMEM((4, 8, rows), F32),
            pltpu.VMEM((n_head, cols, rows), BF16),
            pltpu.VMEM((n_head, cols, rows), BF16),
            pltpu.VMEM((2, 2 * OV * 8, rows), BF16),
            pltpu.VMEM((2, 2 * OV * 8, rows), BF16),
            dma((4,)),
            dma((4,)),
            dma((nz,)),
            dma((nz,)),
            dma((nz,)),
            dma((nz,)),
            dma((4,)),
            dma((4,)),
            dma((n_head,)),
            dma((n_head,)),
            dma((4,)),
            dma((4,)),
            dma((4,)),
            dma((4,)),
            dma((2, n_head)),
            dma((2, n_head)),
            dma((2, n_head)),
            dma((2, n_head)),
            dma((2, n_head)),
            dma((2, n_head)),
            dma((2,)),
            dma((2,)),
        ],
        compiler_params=pltpu.CompilerParams(
            collective_id=0, has_side_effects=True, vmem_limit_bytes=60 * 1024 * 1024
        ),
        cost_estimate=pl.CostEstimate(flops=flops, bytes_accessed=1 << 22, transcendentals=1 << 23),
        name="layer",
    )(tokens, w_qkv, w_out, wdec_t)
    return jnp.transpose(out.reshape(PATCH, w_dec.shape[2], rows), (2, 0, 1))


def solution(mesh):
    return jax.shard_map(
        functools.partial(body, mesh.shape["ctx"], mesh.shape["head"]),
        mesh=mesh,
        in_specs=(P("ctx", None), P(None, None, "head"), P("head", None), P(None, None, "head")),
        out_specs=P("ctx", None, "head"),
        check_vma=False,
    )
```
